32 devices in a mesh: dir: 8 (over z, y), near: 4 (over x, core).
Axes of the slice: x: 2, y: 2, z: 4, core: 2. Of those that a mesh axis runs over, the one named last changes fastest.
Arguments:
- currents: bfloat16 [1024, 128, 128], P(('dir', 'near')), may hold values from -6 to 6
- counts: int32 [32], replicated, may hold values from 0 to 4, as said below
- near_source: int32 [1024, 6], P(('dir', 'near')), may hold values from 0 to 1023, as said below
- near_blocks: bfloat16 [1024, 6, 128, 256], P(('dir', 'near')), may hold values from -0.15625 to 0.15625
- aggregate: bfloat16 [8, 1152, 256], replicated, may hold values from -0.125 to 0.125
- receive: bfloat16 [8, 128, 2304], replicated, may hold values from -0.125 to 0.125
- translations: bfloat16 [1, 1, 1152, 64, 128], P(None, None, ('dir', 'near')), may hold values from -0.5 to 0.5
- source_blocks: int32 [1, 1], replicated, may hold values from 0 to 0, as said below
Outputs:
- fields: bfloat16 [1024, 128, 128], P(('dir', 'near'))
The draws below stay inside these ranges and needn't reach their ends.
Inputs may be any that keep to these rules, and one draw needn't show every extreme that they name: `counts`: devices 2 m and 2 m + 1 of dir and near together (neighbours along near) own exactly 4 parents between them; some device owns 4 and its neighbour none. `near_source`: every entry names a live leaf slot on the device of its row or on a device next to it along near with the same dir index. `source_blocks`: each row names 1 different blocks.
All inputs are finite; a program needn't handle non-finite values.
Results may differ from the reference program's by a relative error of at most 0.005.
Values may be sent and summed in bfloat16 or wider, within the bound.
A program may use at most 128 MiB of HBM per device.

```python
import jax
import jax.numpy as jnp
from jax import lax

P_SIZE = 128
R = 64
K = 1152
NEAR_PER = 6
PAR_SLOTS = 4
BLOCK = 64
PARENTS = 64
LEAF_SLOTS = 32
NBLK = 1
LIST = 1
N_NEAR = 4
DEVICES = 32


def owned_counts(key):
    pair_count = PARENTS // PAR_SLOTS
    first_share = jax.random.randint(jax.random.fold_in(key, 11), (pair_count,), 0, PAR_SLOTS + 1)
    chosen = jax.random.randint(jax.random.fold_in(key, 12), (), 0, pair_count)
    extreme = PAR_SLOTS * jax.random.randint(jax.random.fold_in(key, 13), (), 0, 2)
    first_share = jnp.where(jnp.arange(pair_count) == chosen, extreme, first_share)
    return jnp.stack([first_share, PAR_SLOTS - first_share], axis=1).reshape(-1).astype(jnp.int32)


def draw_counts(key, part):
    return owned_counts(key)


def draw_near_source(key, part):
    counts = owned_counts(key)
    devices = counts.shape[0]
    slot_rows = devices * LEAF_SLOTS
    home_device = jnp.arange(slot_rows, dtype=jnp.int32) // LEAF_SLOTS
    shifts = jnp.array([-1, 0, 1], jnp.int32)
    position = home_device % N_NEAR
    moved_position = position[:, None] + shifts[None, :]
    inside = (moved_position >= 0) & (moved_position < N_NEAR)
    target = jnp.clip(home_device[:, None] + shifts[None, :], 0, devices - 1)
    has_parents = counts[target] > 0
    allowed = inside & has_parents
    scores = jax.random.randint(jax.random.fold_in(key, 21), (slot_rows, NEAR_PER, 3), 0, 1024) * 4 + jnp.arange(3, dtype=jnp.int32)
    scores = jnp.where(allowed[:, None, :], scores, -1)
    picked = jnp.argmax(scores, axis=-1)
    chosen = jnp.take_along_axis(jnp.broadcast_to(target[:, None, :], scores.shape), picked[..., None], axis=-1)[..., 0]
    slot_limit = 8 * counts[chosen]
    slot_drawn = jax.random.randint(jax.random.fold_in(key, 22), (slot_rows, NEAR_PER), 0, slot_limit)
    return (chosen * LEAF_SLOTS + slot_drawn).astype(jnp.int32)


def draw_source_blocks(key, part):
    scores = jax.random.randint(jax.random.fold_in(key, 31), (NBLK, NBLK), 0, 4096) * NBLK + jnp.arange(NBLK, dtype=jnp.int32)[None, :]
    ranked = jnp.argsort(scores, axis=1)
    return ranked[:, :LIST].astype(jnp.int32)


def shard_levels(key, extent, pieces, smallest, top_value):
    gain, own = 1.0, jax.random.fold_in(key, 6)
    for dim, blocks in pieces:
        draws = jnp.exp(jax.random.uniform(jax.random.fold_in(own, dim), (blocks,), jnp.float32, smallest / len(pieces), top_value / len(pieces)))
        gain = gain * jnp.repeat(draws, extent[dim] // blocks).reshape([-1 if axis == dim else 1 for axis in range(len(extent))])
    return gain


def scatter_about(key, shape, width, reach, pieces=(), kind=jnp.bfloat16):
    gain = shard_levels(key, shape, pieces, -0.22, 0.18) if pieces else 1.0
    drawn = jax.random.normal(key, shape, jnp.float32) * width * gain
    return jnp.minimum(jnp.maximum(drawn, -reach), reach).astype(kind)


def setup_inputs(seed: int = 0) -> dict:
    arg_keys = jax.random.split(jax.random.key(seed), 9)
    currents = scatter_about(arg_keys[0], (DEVICES * LEAF_SLOTS, P_SIZE, 2 * R), 1.0, 6.0, ((0, 32),))
    counts = draw_counts(jax.random.fold_in(arg_keys[8], 71), 0)
    near_source = draw_near_source(jax.random.fold_in(arg_keys[8], 71), 0)
    near_blocks = scatter_about(arg_keys[3], (DEVICES * LEAF_SLOTS, NEAR_PER, P_SIZE, 2 * P_SIZE), (2 * P_SIZE * NEAR_PER) ** -0.5, 0.15625, ((0, 32),))
    aggregate = scatter_about(arg_keys[4], (8, K, 2 * P_SIZE), (16 * P_SIZE) ** -0.5, 0.125)
    receive = scatter_about(arg_keys[5], (8, P_SIZE, 2 * K), (2 * K) ** -0.5, 0.125)
    translations = scatter_about(arg_keys[6], (NBLK, LIST, K, BLOCK, 2 * BLOCK), (2 * BLOCK * LIST) ** -0.5, 0.5, ((2, 32),))
    source_blocks = draw_source_blocks(jax.random.fold_in(arg_keys[8], 71), 0)
    return {"currents": currents, "counts": counts, "near_source": near_source, "near_blocks": near_blocks, "aggregate": aggregate, "receive": receive, "translations": translations, "source_blocks": source_blocks}


def turned(values):
    middle = values.shape[-1] // 2
    return jnp.concatenate([-values[..., middle:], values[..., :middle]], axis=-1)


def parent_positions(counts):
    range_ends = jnp.cumsum(counts).astype(jnp.int32)
    parent_ids = jnp.arange(PARENTS, dtype=jnp.int32)
    before = (range_ends[None, :] <= parent_ids[:, None]).astype(jnp.int32)
    owners = jnp.sum(before, axis=1).astype(jnp.int32)
    starts = jnp.sum(before * counts[None, :], axis=1).astype(jnp.int32)
    return (owners * PAR_SLOTS + parent_ids - starts).astype(jnp.int32)


def reference(currents, counts, near_source, near_blocks, aggregate, receive, translations, source_blocks):
    slots = parent_positions(counts)
    leaves = currents.reshape(-1, 8, P_SIZE, 2 * R)
    owned = leaves[slots]
    stacked = jnp.concatenate([owned, turned(owned)], axis=2)
    aggregate_wide = aggregate.astype(jnp.float32)

    def radiate(group_rows):
        return jnp.einsum("ckq,gcqr->gkr", aggregate_wide, group_rows.astype(jnp.float32)).astype(jnp.bfloat16)

    patterns = lax.map(radiate, stacked.reshape(-1, 8, 8, 2 * P_SIZE, 2 * R)).reshape(PARENTS, K, 2 * R)
    blocks = patterns.reshape(NBLK, BLOCK, K, 2 * R)
    with_turned = jnp.concatenate([blocks, turned(blocks)], axis=1)

    def translate(target):
        sources = with_turned[source_blocks[target]].astype(jnp.float32)
        operators = translations[target].astype(jnp.float32)
        return jnp.einsum("lkij,ljkr->ikr", operators, sources).astype(jnp.bfloat16)

    incoming = lax.map(translate, jnp.arange(NBLK, dtype=jnp.int32)).reshape(PARENTS, K, 2 * R)
    receive_wide = receive.astype(jnp.float32)

    def absorb(group_rows):
        doubled = jnp.concatenate([group_rows, turned(group_rows)], axis=1).astype(jnp.float32)
        return jnp.einsum("cpk,gkr->gcpr", receive_wide, doubled)

    far_field = lax.map(absorb, incoming.reshape(-1, 8, K, 2 * R)).reshape(PARENTS * 8, P_SIZE, 2 * R)
    leaf_ids = (slots[:, None] * 8 + jnp.arange(8, dtype=jnp.int32)[None, :]).reshape(-1).astype(jnp.int32)

    def nearby(indices):
        operators = near_blocks[indices].astype(jnp.float32)
        sources = currents[near_source[indices]]
        doubled = jnp.concatenate([sources, turned(sources)], axis=2).astype(jnp.float32)
        return jnp.einsum("genq,geqr->gnr", operators, doubled)

    near_field = lax.map(nearby, leaf_ids.reshape(-1, 64)).reshape(-1, P_SIZE, 2 * R)
    summed = (far_field + near_field).astype(jnp.bfloat16)
    return jnp.zeros(currents.shape, jnp.bfloat16).at[leaf_ids].set(summed)
```

```python
import functools

import jax
import jax.numpy as jnp
from jax import lax
from jax.experimental import pallas as pl
from jax.experimental.pallas import tpu as pltpu
from jax.sharding import PartitionSpec as P

MESH = pl.DeviceIdType.MESH
F32 = jnp.float32
BF16 = jnp.bfloat16


def turned(values):
    width = values.shape[-1]
    rolled = pltpu.roll(values, width // 2, values.ndim - 1)
    lane = lax.broadcasted_iota(jnp.int32, values.shape, values.ndim - 1)
    return jnp.where(lane < width // 2, -rolled, rolled)


def flipped(index, step, count):
    total = 0
    bit = 1
    while bit < count:
        total = total + bit * lax.rem(index // bit + step // bit, 2)
        bit *= 2
    return total


def kernel(
    dims,
    counts,
    near_source,
    source_blocks,
    currents,
    near_blocks,
    aggregate,
    receive,
    translations,
    out,
    own,
    borrowed,
    window,
    near_v,
    agg_v,
    rec_v,
    tra_v,
    stack,
    tile_rows,
    tile_pack,
    send1,
    recv1,
    gathered,
    incoming,
    send2,
    recv2,
    spread,
    joined,
    joined16,
    far_own,
    far_send,
    far_recv,
    near_acc,
    load_sem,
    pair_sem,
    halo_sem,
    a2a_sem,
    far_sem,
):
    dirs, nears, per, padded, slots, dirs_per_tile = dims
    devices = dirs * nears
    leaf_slots = own.shape[0]
    unknowns, channels = own.shape[1:]
    parent_slots = leaf_slots // 8
    half = parent_slots // 2
    near_per = near_v.shape[1]
    directions = agg_v.shape[1]
    dir_index = lax.axis_index("dir")
    near_index = lax.axis_index("near")
    me = dir_index * nears + near_index
    odd = lax.rem(near_index, 2)
    mate = near_index + 1 - 2 * odd
    half_leaves = half * 8

    load_own = pltpu.make_async_copy(currents, own, load_sem.at[0])
    load_agg = pltpu.make_async_copy(aggregate, agg_v, load_sem.at[1])
    load_mid = pltpu.make_async_copy(currents, window.at[pl.ds(leaf_slots, leaf_slots)], load_sem.at[2])
    load_tra = pltpu.make_async_copy(translations, tra_v, load_sem.at[3])
    load_rec = pltpu.make_async_copy(receive, rec_v, load_sem.at[4])
    load_near = pltpu.make_async_copy(near_blocks, near_v, load_sem.at[5])
    load_own.start()
    load_agg.start()

    barrier = pltpu.get_barrier_semaphore()

    def greet(step, carry):
        other = flipped(me, step, devices)
        pl.semaphore_signal(
            barrier, inc=1, device_id=(other // nears, lax.rem(other, nears)), device_id_type=MESH
        )
        return carry

    lax.fori_loop(1, devices, greet, 0)
    pl.semaphore_wait(barrier, devices - 1)

    to_mate = pltpu.make_async_remote_copy(
        src_ref=currents.at[pl.ds((1 - odd) * half_leaves, half_leaves)],
        dst_ref=borrowed,
        send_sem=pair_sem.at[0],
        recv_sem=pair_sem.at[1],
        device_id=(dir_index, mate),
        device_id_type=MESH,
    )
    to_mate.start()

    own_count = counts[me]
    mate_count = counts[dir_index * nears + mate]
    even_count = jnp.where(odd == 0, own_count, mate_count)
    load_own.wait()
    to_mate.wait_recv()
    for w in range(half):
        is_own = jnp.where(odd == 0, w < own_count, half + w >= even_count)
        own_slot = jnp.clip(jnp.where(odd == 0, w, half + w - even_count), 0, parent_slots - 1)
        mate_slot = jnp.clip(jnp.where(odd == 0, w - own_count, w), 0, half - 1)
        for c in range(8):
            mine = own[own_slot * 8 + c].astype(F32)
            theirs = borrowed[mate_slot * 8 + c].astype(F32)
            stack[pl.ds(c * unknowns, unknowns), pl.ds(w * channels, channels)] = jnp.where(
                is_own, mine, theirs
            ).astype(BF16)
    load_agg.wait()
    load_tra.start()
    load_rec.start()
    load_mid.start()
    load_near.start()

    def hop(buffer, target, other, phase):
        return pltpu.make_async_remote_copy(
            src_ref=buffer.at[other],
            dst_ref=target.at[me],
            send_sem=a2a_sem.at[phase, 0],
            recv_sem=a2a_sem.at[phase, 1],
            device_id=(other // nears, lax.rem(other, nears)),
            device_id_type=MESH,
        )

    def all_sent(buffer, phase, which):
        some = buffer.at[pl.ds(0, devices - 1)]
        pltpu.make_async_copy(some, some, a2a_sem.at[phase, which]).wait()

    message = send1.shape[1:]
    tile_devices = dirs_per_tile * nears
    tiles = devices // tile_devices
    rows = tile_devices * per
    block_rows = slots * padded

    def radiate(tile):
        start = pl.multiple_of(tile * rows, 16)
        parts = [agg_v[c, pl.ds(start, rows), :] for c in range(8)]
        real = jnp.concatenate([p[:, :unknowns] for p in parts], axis=1)
        imag = jnp.concatenate([p[:, unknowns:] for p in parts], axis=1)
        rhs = stack[...]
        real = jnp.dot(real, rhs, preferred_element_type=F32)
        imag = jnp.dot(imag, rhs, preferred_element_type=F32)
        for s in range(slots):
            lanes = slice(s * channels, (s + 1) * channels)
            tile_rows[s] = real[:, lanes] + turned(imag[:, lanes])
        for q in range(tile_devices):
            for s in range(slots):
                tile_pack[pl.ds(q * block_rows + s * padded, per), :] = tile_rows[
                    s, pl.ds(q * per, per), :
                ]
        for q in range(tile_devices):
            packed = tile_pack[pl.ds(q * block_rows, block_rows), :]
            send1[tile * tile_devices + q] = packed.reshape(message).astype(BF16)

    my_tile = me // tile_devices

    def radiate_and_send(step, carry):
        tile = flipped(my_tile, tiles - 1 - step, tiles)
        radiate(tile)
        for q in range(tile_devices):
            hop(send1, recv1, tile * tile_devices + q, 0).start()
        return carry

    lax.fori_loop(0, tiles - 1, radiate_and_send, 0)
    radiate(my_tile)
    for q in range(1, tile_devices):
        first = my_tile * tile_devices
        hop(send1, recv1, first + flipped(me - first, q, tile_devices), 0).start()
    recv1[me] = send1[me]

    def halo(side, block):
        return pltpu.make_async_remote_copy(
            src_ref=currents,
            dst_ref=window.at[pl.ds(block * leaf_slots, leaf_slots)],
            send_sem=halo_sem.at[0, block // 2],
            recv_sem=halo_sem.at[1, block // 2],
            device_id=(dir_index, near_index + side),
            device_id_type=MESH,
        )

    @pl.when(near_index < nears - 1)
    def _():
        halo(1, 0).start()

    @pl.when(near_index > 0)
    def _():
        halo(-1, 2).start()

    all_sent(recv1, 0, 1)
    load_tra.wait()
    blocks, listed, _, block_size, doubled = tra_v.shape
    block_len = block_size * padded
    for b in range(blocks):
        per_block = devices // blocks
        got = recv1[pl.ds(b * per_block, per_block)].astype(F32)
        gathered[b] = got.reshape(block_len, channels)

    def translate(k, carry):
        for b in range(blocks):
            summed = None
            for l in range(listed):
                source = 0 if blocks == 1 else source_blocks[b, l]
                rows_k = gathered[source, pl.ds(k, block_size, stride=padded), :]
                both = jnp.concatenate([rows_k, turned(rows_k)], axis=0).astype(BF16)
                part = jnp.dot(tra_v[b, l, k], both, preferred_element_type=F32)
                summed = part if summed is None else summed + part
            incoming[b, pl.ds(k, block_size, stride=padded), :] = summed
        return carry

    lax.fori_loop(0, per, translate, 0, unroll=per % 4 == 0 and per or 1)
    for b in range(blocks):
        per_block = devices // blocks
        packed = incoming[b].reshape((per_block,) + message)
        send2[pl.ds(b * per_block, per_block)] = packed.astype(BF16)

    def send_back(step, carry):
        hop(send2, recv2, flipped(me, devices - 1 - step, devices), 1).start()
        return carry

    lax.fori_loop(0, devices - 1, send_back, 0)
    recv2[me] = send2[me]

    load_mid.wait()
    load_near.wait()

    @pl.when(near_index > 0)
    def _():
        halo(1, 0).wait_recv()

    @pl.when(near_index < nears - 1)
    def _():
        halo(-1, 2).wait_recv()

    base = (me - 1) * leaf_slots

    def nearby(i, carry):
        rows_at = [near_source[i, e] - base for e in range(near_per)]
        sources = [window[jnp.clip(r, 0, 3 * leaf_slots - 1)] for r in rows_at]
        parts = [near_v[i, e] for e in range(near_per)]
        real = jnp.concatenate([p[:, :unknowns] for p in parts], axis=1)
        imag = jnp.concatenate([p[:, unknowns:] for p in parts], axis=1)
        result = jnp.dot(
            jnp.concatenate([real, imag], axis=0),
            jnp.concatenate(sources, axis=0),
            preferred_element_type=F32,
        )
        near_acc[i] = result[:unknowns] + turned(result[unknowns:])
        return carry

    lax.fori_loop(0, leaf_slots, nearby, 0)

    all_sent(recv2, 1, 1)
    load_rec.wait()
    spread[...] = recv2[...].astype(F32).reshape(spread.shape)
    for d in range(devices):
        for s in range(slots):
            joined[pl.ds(d * per, per), pl.ds(s * channels, channels)] = spread[
                pl.ds(d * block_rows + s * padded, per), :
            ]
    joined16[...] = joined[...].astype(BF16)

    def far_copy(c):
        return pltpu.make_async_remote_copy(
            src_ref=far_send.at[c],
            dst_ref=far_recv.at[c],
            send_sem=far_sem.at[0, c],
            recv_sem=far_sem.at[1, c],
            device_id=(dir_index, mate),
            device_id_type=MESH,
        )

    def absorb(c, carry):
        fields = joined16[...]
        real = jnp.dot(rec_v[c, :, pl.ds(0, directions)], fields, preferred_element_type=F32)
        imag = jnp.dot(
            rec_v[c, :, pl.ds(directions, directions)], fields, preferred_element_type=F32
        )
        for s in range(slots):
            lanes = slice(s * channels, (s + 1) * channels)
            far = real[:, lanes] + turned(imag[:, lanes])
            far_own[c, s] = far
            far_send[c, s] = far.astype(BF16)
        far_copy(c).start()
        return carry

    lax.fori_loop(0, 8, absorb, 0)

    def finish(c, carry):
        far_copy(c).wait_recv()
        for s in range(parent_slots):
            place = jnp.where(odd == 0, s, even_count + s)
            mine_at = place - half * odd
            mine = (mine_at >= 0) & (mine_at < half)
            own_at = jnp.clip(mine_at, 0, half - 1)
            mate_at = jnp.clip(place - half * (1 - odd), 0, half - 1)
            theirs = far_recv[c, 0]
            for w in range(1, half):
                theirs = jnp.where(mate_at == w, far_recv[c, w], theirs)
            far = jnp.where(mine, far_own[c, own_at], theirs.astype(F32))
            total = far + near_acc[s * 8 + c]
            out[s * 8 + c] = jnp.where(s < own_count, total, 0.0).astype(BF16)
        return carry

    lax.fori_loop(0, 8, finish, 0)

    to_mate.wait_send()
    all_sent(send1, 0, 0)
    all_sent(send2, 1, 0)
    for c in range(8):
        far_copy(c).wait_send()

    @pl.when(near_index < nears - 1)
    def _():
        halo(1, 0).wait_send()

    @pl.when(near_index > 0)
    def _():
        halo(-1, 2).wait_send()


def body(
    currents, counts, near_source, near_blocks, aggregate, receive, translations, source_blocks
):
    dirs, nears = lax.axis_size("dir"), lax.axis_size("near")
    devices = dirs * nears
    leaf_slots, unknowns, channels = currents.shape
    parent_slots = leaf_slots // 8
    slots = parent_slots // 2
    blocks, listed, per, block_size, doubled = translations.shape
    directions = aggregate.shape[1]
    padded = -(-per * slots // 8) * 8 // slots
    dirs_per_tile = 1
    while dirs_per_tile * nears * per % 16:
        dirs_per_tile *= 2
    rows = dirs_per_tile * nears * per
    message = (slots * padded // 8, 8, channels)
    exchange = pltpu.VMEM((devices,) + message, BF16)
    any_spec = pl.BlockSpec(memory_space=pl.ANY)
    smem_spec = pl.BlockSpec(memory_space=pltpu.SMEM)
    return pl.pallas_call(
        functools.partial(kernel, (dirs, nears, per, padded, slots, dirs_per_tile)),
        out_shape=jax.ShapeDtypeStruct(currents.shape, BF16),
        in_specs=[smem_spec] * 3 + [any_spec] * 5,
        out_specs=pl.BlockSpec(memory_space=pltpu.VMEM),
        scratch_shapes=[
            pltpu.VMEM(currents.shape, BF16),
            pltpu.VMEM((slots * 8, unknowns, channels), BF16),
            pltpu.VMEM((3 * leaf_slots, unknowns, channels), BF16),
            pltpu.VMEM(near_blocks.shape, BF16),
            pltpu.VMEM(aggregate.shape, BF16),
            pltpu.VMEM(receive.shape, BF16),
            pltpu.VMEM(translations.shape, BF16),
            pltpu.VMEM((8 * unknowns, slots * channels), BF16),
            pltpu.VMEM((slots, rows, channels), F32),
            pltpu.VMEM((dirs_per_tile * nears * slots * padded, channels), F32),
            exchange,
            exchange,
            pltpu.VMEM((blocks, block_size * padded, channels), F32),
            pltpu.VMEM((blocks, block_size * padded, channels), F32),
            exchange,
            exchange,
            pltpu.VMEM((devices * slots * padded, channels), F32),
            pltpu.VMEM((directions, slots * channels), F32),
            pltpu.VMEM((directions, slots * channels), BF16),
            pltpu.VMEM((8, slots, unknowns, channels), F32),
            pltpu.VMEM((8, slots, unknowns, channels), BF16),
            pltpu.VMEM((8, slots, unknowns, channels), BF16),
            pltpu.VMEM((leaf_slots, unknowns, channels), F32),
            pltpu.SemaphoreType.DMA((6,)),
            pltpu.SemaphoreType.DMA((2,)),
            pltpu.SemaphoreType.DMA((2, 2)),
            pltpu.SemaphoreType.DMA((2, 2)),
            pltpu.SemaphoreType.DMA((2, 8)),
        ],
        compiler_params=pltpu.CompilerParams(
            collective_id=0, has_side_effects=True, vmem_limit_bytes=60 * 2**20
        ),
    )(
        counts,
        near_source,
        source_blocks,
        currents,
        near_blocks,
        aggregate,
        receive,
        translations,
    )


def solution(mesh):
    return jax.shard_map(
        body,
        mesh=mesh,
        in_specs=(
            P(("dir", "near"), None, None),
            P(),
            P(("dir", "near"), None),
            P(("dir", "near"), None, None, None),
            P(),
            P(),
            P(None, None, ("dir", "near"), None, None),
            P(),
        ),
        out_specs=P(("dir", "near"), None, None),
        check_vma=False,
    )
```

```python
import functools

import jax
import jax.numpy as jnp
from jax import lax
from jax.experimental import pallas as pl
from jax.experimental.pallas import tpu as pltpu
from jax.sharding import PartitionSpec as P

MESH = pl.DeviceIdType.MESH
F32 = jnp.float32
BF16 = jnp.bfloat16


def turned(values):
    width = values.shape[-1]
    rolled = pltpu.roll(values, width // 2, values.ndim - 1)
    lane = lax.broadcasted_iota(jnp.int32, values.shape, values.ndim - 1)
    return jnp.where(lane < width // 2, -rolled, rolled)


def flipped(index, step, count):
    total = 0
    bit = 1
    while bit < count:
        total = total + bit * lax.rem(index // bit + step // bit, 2)
        bit *= 2
    return total


def kernel(
    dims,
    counts,
    near_source,
    source_blocks,
    currents,
    near_blocks,
    aggregate,
    receive,
    translations,
    out,
    own,
    borrowed,
    window,
    near_v,
    agg_v,
    rec_v,
    tra_v,
    stack,
    tile_rows,
    tile_pack,
    send1,
    recv1,
    gathered,
    incoming,
    send2,
    recv2,
    spread,
    joined,
    joined16,
    far_own,
    far_send,
    far_recv,
    near_acc,
    load_sem,
    pair_sem,
    halo_sem,
    a2a_sem,
    far_sem,
):
    dirs, nears, per, padded, slots, dirs_per_tile = dims
    devices = dirs * nears
    leaf_slots = own.shape[0]
    unknowns, channels = own.shape[1:]
    parent_slots = leaf_slots // 8
    half = parent_slots // 2
    near_per = near_v.shape[1]
    directions = agg_v.shape[1]
    dir_index = lax.axis_index("dir")
    near_index = lax.axis_index("near")
    me = dir_index * nears + near_index
    odd = lax.rem(near_index, 2)
    mate = near_index + 1 - 2 * odd
    half_leaves = half * 8

    load_own = pltpu.make_async_copy(currents, own, load_sem.at[0])
    load_agg = pltpu.make_async_copy(aggregate, agg_v, load_sem.at[1])
    load_mid = pltpu.make_async_copy(currents, window.at[pl.ds(leaf_slots, leaf_slots)], load_sem.at[2])
    load_tra = pltpu.make_async_copy(translations, tra_v, load_sem.at[3])
    load_rec = pltpu.make_async_copy(receive, rec_v, load_sem.at[4])
    load_near = pltpu.make_async_copy(near_blocks, near_v, load_sem.at[5])

    def start_pieces(source, target, sem, pieces):
        size = target.shape[0] // pieces
        for piece in range(pieces):
            cut = pl.ds(piece * size, size)
            pltpu.make_async_copy(source.at[cut], target.at[cut], sem).start()

    load_own.start()
    start_pieces(aggregate, agg_v, load_sem.at[1], 8)
    load_tra.start()
    load_mid.start()
    start_pieces(near_blocks, near_v, load_sem.at[5], 8)
    start_pieces(receive, rec_v, load_sem.at[4], 8)

    barrier = pltpu.get_barrier_semaphore()

    def greet(step, carry):
        other = flipped(me, step, devices)
        pl.semaphore_signal(
            barrier, inc=1, device_id=(other // nears, lax.rem(other, nears)), device_id_type=MESH
        )
        return carry

    lax.fori_loop(1, devices, greet, 0)
    pl.semaphore_wait(barrier, devices - 1)

    to_mate = pltpu.make_async_remote_copy(
        src_ref=currents.at[pl.ds((1 - odd) * half_leaves, half_leaves)],
        dst_ref=borrowed,
        send_sem=pair_sem.at[0],
        recv_sem=pair_sem.at[1],
        device_id=(dir_index, mate),
        device_id_type=MESH,
    )
    to_mate.start()

    def halo(side, block):
        return pltpu.make_async_remote_copy(
            src_ref=currents,
            dst_ref=window.at[pl.ds(block * leaf_slots, leaf_slots)],
            send_sem=halo_sem.at[0, block // 2],
            recv_sem=halo_sem.at[1, block // 2],
            device_id=(dir_index, near_index + side),
            device_id_type=MESH,
        )

    @pl.when(near_index < nears - 1)
    def _():
        halo(1, 0).start()

    @pl.when(near_index > 0)
    def _():
        halo(-1, 2).start()

    own_count = counts[me]
    mate_count = counts[dir_index * nears + mate]
    even_count = jnp.where(odd == 0, own_count, mate_count)
    load_own.wait()
    to_mate.wait_recv()
    for w in range(half):
        is_own = jnp.where(odd == 0, w < own_count, half + w >= even_count)
        own_slot = jnp.clip(jnp.where(odd == 0, w, half + w - even_count), 0, parent_slots - 1)
        mate_slot = jnp.clip(jnp.where(odd == 0, w - own_count, w), 0, half - 1)
        for c in range(8):
            mine = own[own_slot * 8 + c].astype(F32)
            theirs = borrowed[mate_slot * 8 + c].astype(F32)
            stack[pl.ds(c * unknowns, unknowns), pl.ds(w * channels, channels)] = jnp.where(
                is_own, mine, theirs
            ).astype(BF16)
    load_agg.wait()

    def hop(buffer, target, other, phase):
        return pltpu.make_async_remote_copy(
            src_ref=buffer.at[other],
            dst_ref=target.at[me],
            send_sem=a2a_sem.at[phase, 0],
            recv_sem=a2a_sem.at[phase, 1],
            device_id=(other // nears, lax.rem(other, nears)),
            device_id_type=MESH,
        )

    def all_sent(buffer, phase, which):
        some = buffer.at[pl.ds(0, devices - 1)]
        pltpu.make_async_copy(some, some, a2a_sem.at[phase, which]).wait()

    message = send1.shape[1:]
    tile_devices = dirs_per_tile * nears
    tiles = devices // tile_devices
    rows = tile_devices * per
    block_rows = slots * padded

    def radiate(tile):
        start = pl.multiple_of(tile * rows, 16)
        parts = [agg_v[c, pl.ds(start, rows), :] for c in range(8)]
        real = jnp.concatenate([p[:, :unknowns] for p in parts], axis=1)
        imag = jnp.concatenate([p[:, unknowns:] for p in parts], axis=1)
        rhs = stack[...]
        real = jnp.dot(real, rhs, preferred_element_type=F32)
        imag = jnp.dot(imag, rhs, preferred_element_type=F32)
        for s in range(slots):
            lanes = slice(s * channels, (s + 1) * channels)
            tile_rows[s] = real[:, lanes] + turned(imag[:, lanes])
        for q in range(tile_devices):
            for s in range(slots):
                tile_pack[pl.ds(q * block_rows + s * padded, per), :] = tile_rows[
                    s, pl.ds(q * per, per), :
                ]
        for q in range(tile_devices):
            packed = tile_pack[pl.ds(q * block_rows, block_rows), :]
            send1[tile * tile_devices + q] = packed.reshape(message).astype(BF16)

    my_tile = me // tile_devices

    def radiate_and_send(step, carry):
        tile = flipped(my_tile, tiles - 1 - step, tiles)
        radiate(tile)
        for q in range(tile_devices):
            hop(send1, recv1, tile * tile_devices + q, 0).start()
        return carry

    lax.fori_loop(0, tiles - 1, radiate_and_send, 0)
    radiate(my_tile)
    for q in range(1, tile_devices):
        first = my_tile * tile_devices
        hop(send1, recv1, first + flipped(me - first, q, tile_devices), 0).start()
    recv1[me] = send1[me]

    all_sent(recv1, 0, 1)
    load_tra.wait()
    blocks, listed, _, block_size, doubled = tra_v.shape
    block_len = block_size * padded
    for b in range(blocks):
        per_block = devices // blocks
        got = recv1[pl.ds(b * per_block, per_block)].astype(F32)
        gathered[b] = got.reshape(block_len, channels)

    def translate(k, carry):
        for b in range(blocks):
            summed = None
            for l in range(listed):
                source = 0 if blocks == 1 else source_blocks[b, l]
                rows_k = gathered[source, pl.ds(k, block_size, stride=padded), :]
                both = jnp.concatenate([rows_k, turned(rows_k)], axis=0).astype(BF16)
                part = jnp.dot(tra_v[b, l, k], both, preferred_element_type=F32)
                summed = part if summed is None else summed + part
            incoming[b, pl.ds(k, block_size, stride=padded), :] = summed
        return carry

    lax.fori_loop(0, per, translate, 0, unroll=per % 4 == 0 and per or 1)
    for b in range(blocks):
        per_block = devices // blocks
        packed = incoming[b].reshape((per_block,) + message)
        send2[pl.ds(b * per_block, per_block)] = packed.astype(BF16)

    def send_back(step, carry):
        hop(send2, recv2, flipped(me, devices - 1 - step, devices), 1).start()
        return carry

    lax.fori_loop(0, devices - 1, send_back, 0)
    recv2[me] = send2[me]

    load_mid.wait()
    load_near.wait()

    @pl.when(near_index > 0)
    def _():
        halo(1, 0).wait_recv()

    @pl.when(near_index < nears - 1)
    def _():
        halo(-1, 2).wait_recv()

    base = (me - 1) * leaf_slots

    def nearby(i, carry):
        rows_at = [near_source[e, i] - base for e in range(near_per)]
        sources = [window[jnp.clip(r, 0, 3 * leaf_slots - 1)] for r in rows_at]
        parts = [near_v[i, e] for e in range(near_per)]
        real = jnp.concatenate([p[:, :unknowns] for p in parts], axis=1)
        imag = jnp.concatenate([p[:, unknowns:] for p in parts], axis=1)
        result = jnp.dot(
            jnp.concatenate([real, imag], axis=0),
            jnp.concatenate(sources, axis=0),
            preferred_element_type=F32,
        )
        near_acc[i] = result[:unknowns] + turned(result[unknowns:])
        return carry

    lax.fori_loop(0, leaf_slots, nearby, 0)

    all_sent(recv2, 1, 1)
    load_rec.wait()
    spread[...] = recv2[...].astype(F32).reshape(spread.shape)
    for d in range(devices):
        for s in range(slots):
            joined[pl.ds(d * per, per), pl.ds(s * channels, channels)] = spread[
                pl.ds(d * block_rows + s * padded, per), :
            ]
    joined16[...] = joined[...].astype(BF16)

    def far_copy(c):
        return pltpu.make_async_remote_copy(
            src_ref=far_send.at[c],
            dst_ref=far_recv.at[c],
            send_sem=far_sem.at[0, c],
            recv_sem=far_sem.at[1, c],
            device_id=(dir_index, mate),
            device_id_type=MESH,
        )

    def absorb(c, carry):
        fields = joined16[...]
        real = jnp.dot(rec_v[c, :, pl.ds(0, directions)], fields, preferred_element_type=F32)
        imag = jnp.dot(
            rec_v[c, :, pl.ds(directions, directions)], fields, preferred_element_type=F32
        )
        for s in range(slots):
            lanes = slice(s * channels, (s + 1) * channels)
            far = real[:, lanes] + turned(imag[:, lanes])
            far_own[c, s] = far
            far_send[c, s] = far.astype(BF16)
        far_copy(c).start()
        return carry

    lax.fori_loop(0, 8, absorb, 0)

    def finish(c, carry):
        far_copy(c).wait_recv()
        for s in range(parent_slots):
            place = jnp.where(odd == 0, s, even_count + s)
            mine_at = place - half * odd
            mine = (mine_at >= 0) & (mine_at < half)
            own_at = jnp.clip(mine_at, 0, half - 1)
            mate_at = jnp.clip(place - half * (1 - odd), 0, half - 1)
            theirs = far_recv[c, 0]
            for w in range(1, half):
                theirs = jnp.where(mate_at == w, far_recv[c, w], theirs)
            far = jnp.where(mine, far_own[c, own_at], theirs.astype(F32))
            total = far + near_acc[s * 8 + c]
            out[s * 8 + c] = jnp.where(s < own_count, total, 0.0).astype(BF16)
        return carry

    lax.fori_loop(0, 8, finish, 0)

    to_mate.wait_send()
    all_sent(send1, 0, 0)
    all_sent(send2, 1, 0)
    for c in range(8):
        far_copy(c).wait_send()

    @pl.when(near_index < nears - 1)
    def _():
        halo(1, 0).wait_send()

    @pl.when(near_index > 0)
    def _():
        halo(-1, 2).wait_send()


def body(
    currents, counts, near_source, near_blocks, aggregate, receive, translations, source_blocks
):
    dirs, nears = lax.axis_size("dir"), lax.axis_size("near")
    devices = dirs * nears
    leaf_slots, unknowns, channels = currents.shape
    parent_slots = leaf_slots // 8
    slots = parent_slots // 2
    blocks, listed, per, block_size, doubled = translations.shape
    directions = aggregate.shape[1]
    padded = -(-per * slots // 8) * 8 // slots
    dirs_per_tile = 1
    while dirs_per_tile * nears * per % 16:
        dirs_per_tile *= 2
    rows = dirs_per_tile * nears * per
    message = (slots * padded // 8, 8, channels)
    exchange = pltpu.VMEM((devices,) + message, BF16)
    any_spec = pl.BlockSpec(memory_space=pl.ANY)
    smem_spec = pl.BlockSpec(memory_space=pltpu.SMEM)
    return pl.pallas_call(
        functools.partial(kernel, (dirs, nears, per, padded, slots, dirs_per_tile)),
        out_shape=jax.ShapeDtypeStruct(currents.shape, BF16),
        in_specs=[smem_spec] * 3 + [any_spec] * 5,
        out_specs=pl.BlockSpec(memory_space=pltpu.VMEM),
        scratch_shapes=[
            pltpu.VMEM(currents.shape, BF16),
            pltpu.VMEM((slots * 8, unknowns, channels), BF16),
            pltpu.VMEM((3 * leaf_slots, unknowns, channels), BF16),
            pltpu.VMEM(near_blocks.shape, BF16),
            pltpu.VMEM(aggregate.shape, BF16),
            pltpu.VMEM(receive.shape, BF16),
            pltpu.VMEM(translations.shape, BF16),
            pltpu.VMEM((8 * unknowns, slots * channels), BF16),
            pltpu.VMEM((slots, rows, channels), F32),
            pltpu.VMEM((dirs_per_tile * nears * slots * padded, channels), F32),
            exchange,
            exchange,
            pltpu.VMEM((blocks, block_size * padded, channels), F32),
            pltpu.VMEM((blocks, block_size * padded, channels), F32),
            exchange,
            exchange,
            pltpu.VMEM((devices * slots * padded, channels), F32),
            pltpu.VMEM((directions, slots * channels), F32),
            pltpu.VMEM((directions, slots * channels), BF16),
            pltpu.VMEM((8, slots, unknowns, channels), F32),
            pltpu.VMEM((8, slots, unknowns, channels), BF16),
            pltpu.VMEM((8, slots, unknowns, channels), BF16),
            pltpu.VMEM((leaf_slots, unknowns, channels), F32),
            pltpu.SemaphoreType.DMA((6,)),
            pltpu.SemaphoreType.DMA((2,)),
            pltpu.SemaphoreType.DMA((2, 2)),
            pltpu.SemaphoreType.DMA((2, 2)),
            pltpu.SemaphoreType.DMA((2, 8)),
        ],
        compiler_params=pltpu.CompilerParams(
            collective_id=0, has_side_effects=True, vmem_limit_bytes=60 * 2**20
        ),
    )(
        counts,
        near_source.T,
        source_blocks,
        currents,
        near_blocks,
        aggregate,
        receive,
        translations,
    )


def solution(mesh):
    return jax.shard_map(
        body,
        mesh=mesh,
        in_specs=(
            P(("dir", "near"), None, None),
            P(),
            P(("dir", "near"), None),
            P(("dir", "near"), None, None, None),
            P(),
            P(),
            P(None, None, ("dir", "near"), None, None),
            P(),
        ),
        out_specs=P(("dir", "near"), None, None),
        check_vma=False,
    )
```

```python
import functools

import jax
import jax.numpy as jnp
from jax import lax
from jax.experimental import pallas as pl
from jax.experimental.pallas import tpu as pltpu
from jax.sharding import PartitionSpec as P

MESH = pl.DeviceIdType.MESH
F32 = jnp.float32
BF16 = jnp.bfloat16


def turned(values):
    width = values.shape[-1]
    rolled = pltpu.roll(values, width // 2, values.ndim - 1)
    lane = lax.broadcasted_iota(jnp.int32, values.shape, values.ndim - 1)
    return jnp.where(lane < width // 2, -rolled, rolled)


def flipped(index, step, count):
    total = 0
    bit = 1
    while bit < count:
        total = total + bit * lax.rem(index // bit + step // bit, 2)
        bit *= 2
    return total


def kernel(
    dims,
    counts,
    near_source,
    source_blocks,
    currents,
    near_blocks,
    aggregate,
    receive,
    translations,
    out,
    own,
    borrowed,
    window,
    near_v,
    agg_v,
    rec_v,
    tra_v,
    stack,
    tile_rows,
    tile_pack,
    send1,
    recv1,
    gathered,
    incoming,
    send2,
    recv2,
    spread,
    joined,
    joined16,
    far_own,
    far_send,
    far_recv,
    near_acc,
    load_sem,
    pair_sem,
    halo_sem,
    a2a_sem,
    far_sem,
):
    dirs, nears, per, padded, slots, dirs_per_tile = dims
    devices = dirs * nears
    leaf_slots = own.shape[0]
    unknowns, channels = own.shape[1:]
    parent_slots = leaf_slots // 8
    half = parent_slots // 2
    near_per = near_v.shape[1]
    directions = agg_v.shape[1]
    dir_index = lax.axis_index("dir")
    near_index = lax.axis_index("near")
    me = dir_index * nears + near_index
    odd = lax.rem(near_index, 2)
    mate = near_index + 1 - 2 * odd
    half_leaves = half * 8

    load_own = pltpu.make_async_copy(currents, own, load_sem.at[0])
    load_agg = pltpu.make_async_copy(aggregate, agg_v, load_sem.at[1])
    load_mid = pltpu.make_async_copy(currents, window.at[pl.ds(leaf_slots, leaf_slots)], load_sem.at[2])
    load_tra = pltpu.make_async_copy(translations, tra_v, load_sem.at[3])
    load_rec = pltpu.make_async_copy(receive, rec_v, load_sem.at[4])
    load_near = pltpu.make_async_copy(near_blocks, near_v, load_sem.at[5])

    def start_pieces(source, target, sem, pieces):
        size = target.shape[0] // pieces
        for piece in range(pieces):
            cut = pl.ds(piece * size, size)
            pltpu.make_async_copy(source.at[cut], target.at[cut], sem).start()

    load_own.start()
    start_pieces(aggregate, agg_v, load_sem.at[1], 8)
    load_tra.start()
    load_mid.start()
    start_pieces(near_blocks, near_v, load_sem.at[5], 8)
    start_pieces(receive, rec_v, load_sem.at[4], 8)

    barrier = pltpu.get_barrier_semaphore()

    def greet(step, carry):
        other = flipped(me, devices - step, devices)
        pl.semaphore_signal(
            barrier, inc=1, device_id=(other // nears, lax.rem(other, nears)), device_id_type=MESH
        )
        return carry

    lax.fori_loop(1, devices, greet, 0, unroll=True)
    pl.semaphore_wait(barrier, devices - 1)

    to_mate = pltpu.make_async_remote_copy(
        src_ref=currents.at[pl.ds((1 - odd) * half_leaves, half_leaves)],
        dst_ref=borrowed,
        send_sem=pair_sem.at[0],
        recv_sem=pair_sem.at[1],
        device_id=(dir_index, mate),
        device_id_type=MESH,
    )
    to_mate.start()

    def halo(side, block):
        return pltpu.make_async_remote_copy(
            src_ref=currents,
            dst_ref=window.at[pl.ds(block * leaf_slots, leaf_slots)],
            send_sem=halo_sem.at[0, block // 2],
            recv_sem=halo_sem.at[1, block // 2],
            device_id=(dir_index, near_index + side),
            device_id_type=MESH,
        )

    @pl.when(near_index < nears - 1)
    def _():
        halo(1, 0).start()

    @pl.when(near_index > 0)
    def _():
        halo(-1, 2).start()

    own_count = counts[me]
    mate_count = counts[dir_index * nears + mate]
    even_count = jnp.where(odd == 0, own_count, mate_count)
    load_own.wait()
    to_mate.wait_recv()
    for w in range(half):
        is_own = jnp.where(odd == 0, w < own_count, half + w >= even_count)
        own_slot = jnp.clip(jnp.where(odd == 0, w, half + w - even_count), 0, parent_slots - 1)
        mate_slot = jnp.clip(jnp.where(odd == 0, w - own_count, w), 0, half - 1)
        for c in range(8):
            mine = own[own_slot * 8 + c].astype(F32)
            theirs = borrowed[mate_slot * 8 + c].astype(F32)
            stack[pl.ds(c * unknowns, unknowns), pl.ds(w * channels, channels)] = jnp.where(
                is_own, mine, theirs
            ).astype(BF16)
    load_agg.wait()

    def hop(buffer, target, other, phase):
        return pltpu.make_async_remote_copy(
            src_ref=buffer.at[other],
            dst_ref=target.at[me],
            send_sem=a2a_sem.at[phase, 0],
            recv_sem=a2a_sem.at[phase, 1],
            device_id=(other // nears, lax.rem(other, nears)),
            device_id_type=MESH,
        )

    def all_sent(buffer, phase, which):
        some = buffer.at[pl.ds(0, devices - 1)]
        pltpu.make_async_copy(some, some, a2a_sem.at[phase, which]).wait()

    message = send1.shape[1:]
    tile_devices = dirs_per_tile * nears
    tiles = devices // tile_devices
    rows = tile_devices * per
    block_rows = slots * padded

    def radiate(tile):
        start = pl.multiple_of(tile * rows, 16)
        parts = [agg_v[c, pl.ds(start, rows), :] for c in range(8)]
        real = jnp.concatenate([p[:, :unknowns] for p in parts], axis=1)
        imag = jnp.concatenate([p[:, unknowns:] for p in parts], axis=1)
        rhs = stack[...]
        real = jnp.dot(real, rhs, preferred_element_type=F32)
        imag = jnp.dot(imag, rhs, preferred_element_type=F32)
        for s in range(slots):
            lanes = slice(s * channels, (s + 1) * channels)
            tile_rows[s] = real[:, lanes] + turned(imag[:, lanes])
        for q in range(tile_devices):
            for s in range(slots):
                tile_pack[pl.ds(q * block_rows + s * padded, per), :] = tile_rows[
                    s, pl.ds(q * per, per), :
                ]
        for q in range(tile_devices):
            packed = tile_pack[pl.ds(q * block_rows, block_rows), :]
            send1[tile * tile_devices + q] = packed.reshape(message).astype(BF16)

    my_tile = me // tile_devices

    def radiate_and_send(step, carry):
        tile = flipped(my_tile, tiles - 1 - step, tiles)
        radiate(tile)
        for q in range(tile_devices):
            hop(send1, recv1, tile * tile_devices + q, 0).start()
        return carry

    lax.fori_loop(0, tiles - 1, radiate_and_send, 0)
    radiate(my_tile)
    for q in range(1, tile_devices):
        first = my_tile * tile_devices
        hop(send1, recv1, first + flipped(me - first, q, tile_devices), 0).start()
    recv1[me] = send1[me]

    all_sent(recv1, 0, 1)
    load_tra.wait()
    blocks, listed, _, block_size, doubled = tra_v.shape
    block_len = block_size * padded
    for b in range(blocks):
        per_block = devices // blocks
        got = recv1[pl.ds(b * per_block, per_block)].astype(F32)
        gathered[b] = got.reshape(block_len, channels)

    def translate(k, carry):
        for b in range(blocks):
            summed = None
            for l in range(listed):
                source = 0 if blocks == 1 else source_blocks[b, l]
                rows_k = gathered[source, pl.ds(k, block_size, stride=padded), :]
                both = jnp.concatenate([rows_k, turned(rows_k)], axis=0).astype(BF16)
                part = jnp.dot(tra_v[b, l, k], both, preferred_element_type=F32)
                summed = part if summed is None else summed + part
            incoming[b, pl.ds(k, block_size, stride=padded), :] = summed
        return carry

    lax.fori_loop(0, per, translate, 0, unroll=per % 4 == 0 and per or 1)
    for b in range(blocks):
        per_block = devices // blocks
        packed = incoming[b].reshape((per_block,) + message)
        send2[pl.ds(b * per_block, per_block)] = packed.astype(BF16)

    def send_back(step, carry):
        hop(send2, recv2, flipped(me, devices - 1 - step, devices), 1).start()
        return carry

    lax.fori_loop(0, devices - 1, send_back, 0, unroll=True)
    recv2[me] = send2[me]

    load_mid.wait()
    load_near.wait()

    @pl.when(near_index > 0)
    def _():
        halo(1, 0).wait_recv()

    @pl.when(near_index < nears - 1)
    def _():
        halo(-1, 2).wait_recv()

    base = (me - 1) * leaf_slots

    def nearby(i, carry):
        rows_at = [near_source[e, i] - base for e in range(near_per)]
        sources = [window[jnp.clip(r, 0, 3 * leaf_slots - 1)] for r in rows_at]
        parts = [near_v[i, e] for e in range(near_per)]
        real = jnp.concatenate([p[:, :unknowns] for p in parts], axis=1)
        imag = jnp.concatenate([p[:, unknowns:] for p in parts], axis=1)
        result = jnp.dot(
            jnp.concatenate([real, imag], axis=0),
            jnp.concatenate(sources, axis=0),
            preferred_element_type=F32,
        )
        near_acc[i] = result[:unknowns] + turned(result[unknowns:])
        return carry

    lax.fori_loop(0, leaf_slots, nearby, 0)

    all_sent(recv2, 1, 1)
    load_rec.wait()
    spread[...] = recv2[...].astype(F32).reshape(spread.shape)
    for d in range(devices):
        for s in range(slots):
            joined[pl.ds(d * per, per), pl.ds(s * channels, channels)] = spread[
                pl.ds(d * block_rows + s * padded, per), :
            ]
    joined16[...] = joined[...].astype(BF16)

    def far_copy(c):
        return pltpu.make_async_remote_copy(
            src_ref=far_send.at[c],
            dst_ref=far_recv.at[c],
            send_sem=far_sem.at[0, c],
            recv_sem=far_sem.at[1, c],
            device_id=(dir_index, mate),
            device_id_type=MESH,
        )

    def absorb(c, carry):
        fields = joined16[...]
        real = jnp.dot(rec_v[c, :, pl.ds(0, directions)], fields, preferred_element_type=F32)
        imag = jnp.dot(
            rec_v[c, :, pl.ds(directions, directions)], fields, preferred_element_type=F32
        )
        for s in range(slots):
            lanes = slice(s * channels, (s + 1) * channels)
            far = real[:, lanes] + turned(imag[:, lanes])
            far_own[c, s] = far
            far_send[c, s] = far.astype(BF16)
        far_copy(c).start()
        return carry

    lax.fori_loop(0, 8, absorb, 0)

    def finish(c, carry):
        far_copy(c).wait_recv()
        for s in range(parent_slots):
            place = jnp.where(odd == 0, s, even_count + s)
            mine_at = place - half * odd
            mine = (mine_at >= 0) & (mine_at < half)
            own_at = jnp.clip(mine_at, 0, half - 1)
            mate_at = jnp.clip(place - half * (1 - odd), 0, half - 1)
            theirs = far_recv[c, 0]
            for w in range(1, half):
                theirs = jnp.where(mate_at == w, far_recv[c, w], theirs)
            far = jnp.where(mine, far_own[c, own_at], theirs.astype(F32))
            total = far + near_acc[s * 8 + c]
            out[s * 8 + c] = jnp.where(s < own_count, total, 0.0).astype(BF16)
        return carry

    lax.fori_loop(0, 8, finish, 0)

    to_mate.wait_send()
    all_sent(send1, 0, 0)
    all_sent(send2, 1, 0)
    for c in range(8):
        far_copy(c).wait_send()

    @pl.when(near_index < nears - 1)
    def _():
        halo(1, 0).wait_send()

    @pl.when(near_index > 0)
    def _():
        halo(-1, 2).wait_send()


def body(
    currents, counts, near_source, near_blocks, aggregate, receive, translations, source_blocks
):
    dirs, nears = lax.axis_size("dir"), lax.axis_size("near")
    devices = dirs * nears
    leaf_slots, unknowns, channels = currents.shape
    parent_slots = leaf_slots // 8
    slots = parent_slots // 2
    blocks, listed, per, block_size, doubled = translations.shape
    directions = aggregate.shape[1]
    padded = -(-per * slots // 8) * 8 // slots
    dirs_per_tile = 1
    while dirs_per_tile * nears * per % 16:
        dirs_per_tile *= 2
    rows = dirs_per_tile * nears * per
    message = (slots * padded // 8, 8, channels)
    exchange = pltpu.VMEM((devices,) + message, BF16)
    any_spec = pl.BlockSpec(memory_space=pl.ANY)
    smem_spec = pl.BlockSpec(memory_space=pltpu.SMEM)
    return pl.pallas_call(
        functools.partial(kernel, (dirs, nears, per, padded, slots, dirs_per_tile)),
        out_shape=jax.ShapeDtypeStruct(currents.shape, BF16),
        in_specs=[smem_spec] * 3 + [any_spec] * 5,
        out_specs=pl.BlockSpec(memory_space=pltpu.VMEM),
        scratch_shapes=[
            pltpu.VMEM(currents.shape, BF16),
            pltpu.VMEM((slots * 8, unknowns, channels), BF16),
            pltpu.VMEM((3 * leaf_slots, unknowns, channels), BF16),
            pltpu.VMEM(near_blocks.shape, BF16),
            pltpu.VMEM(aggregate.shape, BF16),
            pltpu.VMEM(receive.shape, BF16),
            pltpu.VMEM(translations.shape, BF16),
            pltpu.VMEM((8 * unknowns, slots * channels), BF16),
            pltpu.VMEM((slots, rows, channels), F32),
            pltpu.VMEM((dirs_per_tile * nears * slots * padded, channels), F32),
            exchange,
            exchange,
            pltpu.VMEM((blocks, block_size * padded, channels), F32),
            pltpu.VMEM((blocks, block_size * padded, channels), F32),
            exchange,
            exchange,
            pltpu.VMEM((devices * slots * padded, channels), F32),
            pltpu.VMEM((directions, slots * channels), F32),
            pltpu.VMEM((directions, slots * channels), BF16),
            pltpu.VMEM((8, slots, unknowns, channels), F32),
            pltpu.VMEM((8, slots, unknowns, channels), BF16),
            pltpu.VMEM((8, slots, unknowns, channels), BF16),
            pltpu.VMEM((leaf_slots, unknowns, channels), F32),
            pltpu.SemaphoreType.DMA((6,)),
            pltpu.SemaphoreType.DMA((2,)),
            pltpu.SemaphoreType.DMA((2, 2)),
            pltpu.SemaphoreType.DMA((2, 2)),
            pltpu.SemaphoreType.DMA((2, 8)),
        ],
        compiler_params=pltpu.CompilerParams(
            collective_id=0, has_side_effects=True, vmem_limit_bytes=60 * 2**20
        ),
    )(
        counts,
        near_source.T,
        source_blocks,
        currents,
        near_blocks,
        aggregate,
        receive,
        translations,
    )


def solution(mesh):
    return jax.shard_map(
        body,
        mesh=mesh,
        in_specs=(
            P(("dir", "near"), None, None),
            P(),
            P(("dir", "near"), None),
            P(("dir", "near"), None, None, None),
            P(),
            P(),
            P(None, None, ("dir", "near"), None, None),
            P(),
        ),
        out_specs=P(("dir", "near"), None, None),
        check_vma=False,
    )
```
